32 devices in a mesh: shot: 8 (over z, x), sub: 4 (over y, core).
Axes of the slice: x: 2, y: 2, z: 4, core: 2. Of those that a mesh axis runs over, the one named last changes fastest.
Arguments:
- courant: float32 [8, 128, 128, 128], P('shot', 'sub'), may hold values from 0.04 to 0.2
- adjoint_prev: float32 [8, 128, 128, 128], P('shot', 'sub'), may hold values from -6 to 6
- adjoint_now: float32 [8, 128, 128, 128], P('shot', 'sub'), may hold values from -6 to 6
- forward_accel: float32 [8, 4, 128, 128, 128], P('shot', None, 'sub'), may hold values from -6 to 6
- traces: float32 [8, 4, 512], P('shot'), may hold values from -24 to 24
- receivers: int32 [8, 512], P('shot'), may hold values from 0 to 2097151
- owners: int32 [8, 4, 16, 1], P('shot', 'sub'), may hold values from 0 to 7; in each aligned block of 16 rows (0 to 15, 16 to 31, ..., all dimensions but the last counted through in order) at most 2 rows name the same one
- tile_slot: int32 [8, 4, 16], P('shot', 'sub'), may hold values from 0 to 7
Outputs:
- smoothed: float32 [64, 128, 8, 128], P('shot', 'sub')
- adjoint_last: float32 [8, 128, 128, 128], P('shot', 'sub')
The draws below stay inside these ranges and needn't reach their ends.
Inputs may be any that keep to these rules, and one draw needn't show every extreme that they name: `owners`: among the 16 blocks of one device at most 2 name the same owner, and in some device's blocks one owner is named by exactly 2.
All inputs are finite; a program needn't handle non-finite values.
Results may differ from the reference program's by a relative error of at most 0.00013.
Values sent between devices are 32-bit elements; how exact they have to be, the bound alone decides.
A program may use at most 128 MiB of HBM per device.

```python
import math
import jax
import jax.numpy as jnp
import numpy as np
from jax import lax

ZD = 32
AX = 128
AY = 128
TX = 8
TILES_OWN = 8
CAP = 2
STEPS = 4
NREC = 512
Z = 128
KB = 16
NT = 64
N_SHOT = 8
N_SUB = 4


def with_ends(array, own_key, least, largest):
    index_at = [jax.random.randint(jax.random.fold_in(own_key, axis), (), 0, length) for axis, length in enumerate(array.shape)]
    main_axis = array.shape.index(max(array.shape))
    neighbour = index_at[:main_axis] + [(index_at[main_axis] + 1) % array.shape[main_axis]] + index_at[main_axis + 1:]
    return array.at[tuple(index_at)].set(least).at[tuple(neighbour)].set(largest)


def block_scale(own_key, dims, shards, smallest, high):
    level, own = 1.0, jax.random.fold_in(own_key, 6)
    for position, blocks in shards:
        steps = jnp.exp(jax.random.uniform(jax.random.fold_in(own, position), (blocks,), jnp.float32, smallest / len(shards), high / len(shards)))
        level = level * jnp.repeat(steps, dims[position] // blocks).reshape([-1 if axis == position else 1 for axis in range(len(dims))])
    return level


def routed_block(rng, own, number, rows, amount, top, bound, skew):
    sequence = jax.random.permutation(rng, amount)
    crowded, ordinary = load_shares(amount, rows * top, bound, skew, True), load_shares(amount, rows * top, bound, skew, False)
    places = jnp.arange(amount)

    def named(tallies, rotation):
        used = int((tallies > 0).sum())
        fixed = max(1, used // 4)
        moved = fixed + (places - fixed + rotation * (used - fixed)) % max(1, amount - fixed)
        return jnp.zeros((amount,), jnp.int32).at[sequence[jnp.where(places < fixed, places, moved)]].set(jnp.asarray(tallies, jnp.int32))

    tallies = jnp.where(number % 4 == 0, named(crowded, number // 4), named(ordinary, number - number // 4 - 1))
    mixed = jax.random.permutation(jax.random.fold_in(own, 3), amount)
    donor, sink = mixed[0:amount // 2 * 2:2], mixed[1:amount // 2 * 2:2]
    slack = jnp.minimum(tallies[donor] - 1, bound - tallies[sink]) // 2
    slack = jnp.where((donor == sequence[0]) | (sink == sequence[0]) | (tallies[sink] == 0), 0, jnp.maximum(slack, 0))
    moved = jax.random.randint(jax.random.fold_in(own, 4), (amount // 2,), 0, 1 << 20) % (slack + 1)
    tallies = tallies.at[donor].add(-moved).at[sink].add(moved)
    labels = jnp.searchsorted(jnp.cumsum(tallies), jnp.arange(rows * top), side="right").astype(jnp.int32)
    grid = labels.reshape(top, rows).T
    grid = grid[jax.random.permutation(jax.random.fold_in(own, 1), rows)]
    rotation = jax.random.randint(jax.random.fold_in(own, 2), (rows, 1), 0, top)
    return jnp.take_along_axis(grid, (jnp.arange(top)[None, :] + rotation) % top, axis=1)


def load_shares(number_of, total, limit, lean, full):
    weights = [(1 << 20) // math.isqrt(rank ** lean) + 1 for rank in range(1, number_of + 1)]
    largest = limit if full else min(limit, max(-(-total // number_of), total * weights[0] // sum(weights)))
    least = 1 if total - largest >= number_of - 1 else 0
    counts, spare = [largest] + [least] * (number_of - 1), total - largest - least * (number_of - 1)
    while spare > 0:
        free = [i for i in range(1, number_of) if counts[i] < largest] or [i for i in range(1, number_of) if counts[i] < limit]
        pool, left = sum([weights[i] for i in free]), spare
        for i in free:
            extra = min(limit - counts[i], max(1, left * weights[i] // pool), spare)
            counts[i] = counts[i] + extra
            spare = spare - extra
    return np.array(counts)


def centred(key, extent, scale, bound, split=(), kind=jnp.bfloat16):
    factor_of = block_scale(key, extent, split, -0.22, 0.18) if split else 1.0
    result = jax.random.normal(key, extent, jnp.float32) * scale * factor_of
    return jnp.minimum(jnp.maximum(result, -bound), bound).astype(kind)


def setup_inputs(seed: int = 0) -> dict:
    splits = jax.random.split(jax.random.key(seed), 9)
    courant = jnp.clip(jnp.exp(math.log(0.2) - 1.609438 * jax.random.uniform(splits[0], (N_SHOT, Z, AX, AY), jnp.float32) ** block_scale(splits[0], (N_SHOT, Z, AX, AY), ((0, 8), (1, 4)), -0.2, 0.2)), 0.04, 0.2)
    adjoint_prev = centred(splits[1], (N_SHOT, Z, AX, AY), 1.0, 6.0, ((0, 8), (1, 4)), jnp.float32)
    adjoint_now = centred(splits[2], (N_SHOT, Z, AX, AY), 1.0, 6.0, ((0, 8), (1, 4)), jnp.float32)
    forward_accel = centred(splits[3], (N_SHOT, STEPS, Z, AX, AY), 1.0, 6.0, ((0, 8), (2, 4)), jnp.float32)
    traces = centred(splits[4], (N_SHOT, STEPS, NREC), 4.0, 24.0, ((0, 8),), jnp.float32)
    receivers = with_ends(jax.random.randint(splits[5], (N_SHOT, NREC), 0, Z * AX * AY), jax.random.fold_in(splits[5], 1), 0, (Z * AX * AY) - 1).astype(jnp.int32)
    owners_keys = jax.random.split(jax.random.fold_in(splits[6], 1), N_SHOT * N_SUB * KB // KB)
    owners_turns = jax.random.permutation(jax.random.fold_in(splits[6], 3), N_SHOT * N_SUB * KB // KB)
    owners = jax.vmap(lambda own, number: routed_block(jax.random.fold_in(splits[6], 2), own, number, KB, N_SHOT, 1, CAP, 2))(owners_keys, owners_turns).reshape((N_SHOT, N_SUB, KB, 1))
    tile_slot = with_ends(jax.random.randint(splits[7], (N_SHOT, N_SUB, KB), 0, TILES_OWN), jax.random.fold_in(splits[7], 1), 0, TILES_OWN - 1).astype(jnp.int32)
    return {"courant": courant, "adjoint_prev": adjoint_prev, "adjoint_now": adjoint_now, "forward_accel": forward_accel, "traces": traces, "receivers": receivers, "owners": owners, "tile_slot": tile_slot}


stencil_weights = (-205.0 / 72.0, 8.0 / 5.0, -1.0 / 5.0, 8.0 / 315.0, -1.0 / 560.0)


def laplace_eight(padded, depth_len, rows_x, cols_y):
    centre = padded[4:4 + depth_len, 4:4 + rows_x, 4:4 + cols_y]
    summed = 3.0 * stencil_weights[0] * centre
    for distance in range(1, 5):
        factor = stencil_weights[distance]
        pairs = padded[4 + distance:4 + distance + depth_len, 4:4 + rows_x, 4:4 + cols_y]
        pairs = pairs + padded[4 - distance:4 - distance + depth_len, 4:4 + rows_x, 4:4 + cols_y]
        pairs = pairs + padded[4:4 + depth_len, 4 + distance:4 + distance + rows_x, 4:4 + cols_y]
        pairs = pairs + padded[4:4 + depth_len, 4 - distance:4 - distance + rows_x, 4:4 + cols_y]
        pairs = pairs + padded[4:4 + depth_len, 4:4 + rows_x, 4 + distance:4 + distance + cols_y]
        pairs = pairs + padded[4:4 + depth_len, 4:4 + rows_x, 4 - distance:4 - distance + cols_y]
        summed = summed + factor * pairs
    return summed


def band_matrix(depth_len, band_reach):
    row_ids = jnp.arange(depth_len)[:, None]
    col_ids = jnp.arange(depth_len)[None, :]
    distance = (row_ids - col_ids).astype(jnp.float32)
    weights = jnp.where(jnp.abs(row_ids - col_ids) <= band_reach, jnp.exp(-(2.0 * distance / band_reach) ** 2), 0.0)
    return weights / jnp.sum(weights, axis=1, keepdims=True)


def propagate(inputs):
    speed, previous, current, accel, trace, receiver = inputs
    gradient = jnp.zeros_like(current)
    for time_step in range(STEPS):
        padded = jnp.pad(current, 4)
        advanced = 2.0 * current - previous + speed * laplace_eight(padded, Z, AX, AY)
        advanced = advanced.reshape(-1).at[receiver].add(trace[time_step]).reshape(current.shape)
        gradient = gradient + advanced * accel[time_step]
        previous, current = current, advanced
    return current, gradient


def slab_sum(blocks, tile_ids):
    return jax.ops.segment_sum(blocks, tile_ids, num_segments=NT)


def reference(courant, adjoint_prev, adjoint_now, forward_accel, traces, receivers, owners, tile_slot):
    adjoint_last, gradients = lax.map(propagate, (courant, adjoint_prev, adjoint_now, forward_accel, traces, receivers))
    blocks = gradients.reshape(N_SHOT, N_SUB, ZD, KB, TX, AY).transpose(1, 0, 3, 2, 4, 5).reshape(N_SUB, N_SHOT * KB, ZD, TX, AY)
    tile_ids = (owners[:, :, :, 0] * TILES_OWN + tile_slot).transpose(1, 0, 2).reshape(N_SUB, N_SHOT * KB).astype(jnp.int32)
    per_slab = jax.vmap(slab_sum)(blocks, tile_ids)
    model = per_slab.transpose(1, 0, 2, 3, 4).reshape(NT, Z, TX, AY)
    smoothed = jnp.einsum('ij,tjxy->tixy', band_matrix(Z, ZD), model, precision=lax.Precision.HIGHEST)
    return smoothed, adjoint_last
```

```python
import functools

import jax
import jax.numpy as jnp
from jax import lax
from jax.experimental import pallas as pl
from jax.experimental.pallas import tpu as pltpu
from jax.sharding import PartitionSpec as P

TX = 8
TILES_OWN = 8
CAP = 2
HALO = 4
PAD = 8
UNROLL = 4
MESH = pl.DeviceIdType.MESH

stencil_weights = (-205.0 / 72.0, 8.0 / 5.0, -1.0 / 5.0, 8.0 / 315.0, -1.0 / 560.0)


def prepare_kernel(slab_cells, cols_y, rec_ref, tr_ref, own_ref, slot_ref, src_ref, inv_ref, ids_ref, count_ref):
    steps = tr_ref.shape[1]
    spare = slab_cells // cols_y
    zrows = 256

    def zero(i, _):
        src_ref[pl.ds(pl.multiple_of(i * zrows, zrows), zrows), :] = jnp.zeros((zrows, cols_y), jnp.float32)
        return 0

    lax.fori_loop(0, spare * steps // zrows, zero, 0)
    base = lax.axis_index("sub") * slab_cells
    lane = lax.broadcasted_iota(jnp.int32, (steps, cols_y), 1)
    group = 128

    def add(g, _):
        first = pl.multiple_of(g * group, group)
        values = tr_ref[0, :, pl.ds(first, group)]
        for r in range(group):
            off = rec_ref[0, first + r] - base
            inside = (off >= 0) & (off < slab_cells)
            row = jnp.where(inside, lax.div(off, cols_y), spare)
            at = pl.ds(pl.multiple_of(row * steps, steps), steps)
            value = jnp.broadcast_to(values[:, r : r + 1], (steps, cols_y))
            src_ref[at, :] += jnp.where(lane == lax.rem(off, cols_y), value, 0.0)
        return 0

    lax.fori_loop(0, rec_ref.shape[1] // group, add, 0)

    ids_ref[...] = jnp.full(ids_ref.shape, -1, jnp.int32)
    for i in range(count_ref.shape[0]):
        count_ref[i] = 0
    for i in range(inv_ref.shape[0]):
        inv_ref[i] = 0
    for k in range(slot_ref.shape[0]):
        owner = own_ref[k]
        place = owner * CAP + count_ref[owner]
        count_ref[owner] = count_ref[owner] + 1
        inv_ref[place] = k
        ids_ref[pl.ds(place, 1)] = jnp.full((1,) + ids_ref.shape[1:], slot_ref[k], jnp.int32)


def adjoint_kernel(
    n_shot, n_sub, inv_ref, ids_ref, src_ref, cour_hbm, prev_hbm, now_hbm, acc_hbm,
    last_hbm, out_hbm,
    even, odd, cour, acc, grad, packed, recv, rids, tiles, smooth, taps, scale,
    lsem, asem, hsend, hrecv, isend, irecv, dsend, drecv, nsend, nrecv, fsem, osem,
):
    buf = (even, odd)
    shot, sub = lax.axis_index("shot"), lax.axis_index("sub")
    steps, depth, rows, cols = acc.shape
    places = packed.shape[1]
    chunk = HALO
    chunks = depth // chunk
    inner = pl.ds(PAD, rows)
    rising = lax.rem(sub, 2)
    front, back = sub + 1 - 2 * rising, sub - 1 + 2 * rising
    has_front = (front >= 0) & (front < n_sub)
    has_back = (back >= 0) & (back < n_sub)
    has_low, has_high = sub > 0, sub < n_sub - 1

    def slab(j):
        return chunk * (rising * j + (1 - rising) * (chunks - 1 - j))

    def load(which, j):
        part = pl.ds(slab(j), chunk)
        inside = pl.ds(slab(j) + HALO, chunk)
        if which == 0:
            return pltpu.make_async_copy(now_hbm.at[0, part], even.at[inside, inner, :], lsem.at[0, j])
        if which == 1:
            return pltpu.make_async_copy(prev_hbm.at[0, part], odd.at[inside, inner, :], lsem.at[1, j])
        return pltpu.make_async_copy(cour_hbm.at[0, part], cour.at[part], lsem.at[2, j])

    def load_acc(t, j):
        part = pl.ds(slab(j), chunk)
        return pltpu.make_async_copy(acc_hbm.at[0, t, part], acc.at[t, part], asem.at[t, j])

    load(0, 0).start()
    for i in range(chunks + steps - 1):
        for t in range(steps):
            j = i - t
            if 0 <= j < chunks:
                if t == 0:
                    if j + 1 < chunks:
                        load(0, j + 1).start()
                    load(1, j).start()
                    load(2, j).start()
                load_acc(t, j).start()

    barrier = pltpu.get_barrier_semaphore()

    def peer_of(m):
        return lax.rem(shot + m, n_shot)

    for m in range(1, n_shot):
        pl.semaphore_signal(barrier, inc=1, device_id={"shot": peer_of(m)}, device_id_type=MESH)

    @pl.when(has_front)
    def _():
        pl.semaphore_signal(barrier, inc=1, device_id={"sub": front}, device_id_type=MESH)

    @pl.when(has_back)
    def _():
        pl.semaphore_signal(barrier, inc=1, device_id={"sub": back}, device_id_type=MESH)

    for ref in buf:
        for rim in (0, PAD + rows):
            ref[HALO : HALO + depth, rim : rim + PAD, :] = jnp.zeros((depth, PAD, cols), jnp.float32)

    def clear(first):
        for ref in buf:
            ref[first : first + HALO, inner, :] = jnp.zeros((HALO, rows, cols), jnp.float32)

    @pl.when(jnp.logical_not(has_low))
    def _():
        clear(0)

    @pl.when(jnp.logical_not(has_high))
    def _():
        clear(HALO + depth)

    near = jnp.minimum(sub, 1) + jnp.minimum(n_sub - 1 - sub, 1)
    pl.semaphore_wait(barrier, n_shot - 1 + near)

    def halo(t, side):
        b = buf[t % 2]
        if side == 0:
            first, land, device = (1 - rising) * (depth - HALO), rising * (depth + HALO), front
        else:
            first, land, device = rising * (depth - HALO), (1 - rising) * (depth + HALO), back
        source = now_hbm.at[0, pl.ds(first, HALO)] if t == 0 else b.at[pl.ds(first + HALO, HALO), inner, :]
        return pltpu.make_async_remote_copy(
            src_ref=source, dst_ref=b.at[pl.ds(land, HALO), inner, :],
            send_sem=hsend.at[t, side], recv_sem=hrecv.at[t, side],
            device_id={"sub": device}, device_id_type=MESH,
        )

    there = (has_front, has_back)

    def start_halo(t, side):
        @pl.when(there[side])
        def _():
            halo(t, side).start()

    def wait_halo(t, side):
        @pl.when(there[side])
        def _():
            halo(t, side).wait()

    start_halo(0, 0)
    start_halo(0, 1)

    def ids_copy(m):
        peer = peer_of(m)
        return pltpu.make_async_remote_copy(
            src_ref=ids_ref.at[pl.ds(CAP * peer, CAP)], dst_ref=rids.at[pl.ds(CAP * m, CAP)],
            send_sem=isend.at[m], recv_sem=irecv.at[m],
            device_id={"shot": peer}, device_id_type=MESH,
        )

    def data_copy(j, m):
        peer = peer_of(m)
        return pltpu.make_async_remote_copy(
            src_ref=packed.at[j, pl.ds(CAP * peer, CAP)], dst_ref=recv.at[j, pl.ds(CAP * m, CAP)],
            send_sem=dsend.at[j, m], recv_sem=drecv.at[j, m],
            device_id={"shot": peer}, device_id_type=MESH,
        )

    for m in range(1, n_shot):
        ids_copy(m).start()

    lane = lax.broadcasted_iota(jnp.int32, (TX, cols), 1)
    from_left = [None] + [jnp.where(lane >= d, stencil_weights[d], 0.0) for d in range(1, 5)]
    from_right = [None] + [jnp.where(lane < cols - d, stencil_weights[d], 0.0) for d in range(1, 5)]

    def advance(t, j):
        cur, nxt = buf[t % 2], buf[(t + 1) % 2]
        z0 = slab(j)

        def block(i, _):
            for u in range(UNROLL):
                xb = i * UNROLL + u
                x0 = pl.multiple_of(xb * TX, TX)
                own = pl.ds(x0, TX)
                here = pl.ds(pl.multiple_of(x0 + PAD, TX), TX)
                col = {k: cur[z0 + (k + HALO), here, :] for k in range(-HALO, chunk + HALO)}
                for k in range(chunk):
                    z = z0 + k
                    c = col[k]
                    lap = (3.0 * stencil_weights[0]) * c
                    for d in range(1, 5):
                        pair = (col[k + d] + col[k - d]) + (
                            cur[z + HALO, pl.ds(x0 + (PAD + d), TX), :]
                            + cur[z + HALO, pl.ds(x0 + (PAD - d), TX), :]
                        )
                        lap = lap + stencil_weights[d] * pair
                        lap = lap + from_left[d] * pltpu.roll(c, d, 1)
                        lap = lap + from_right[d] * pltpu.roll(c, cols - d, 1)
                    source = src_ref[pl.ds((z * rows + x0) * steps + t, TX, stride=steps), :]
                    adv = (2.0 * c - nxt[z + HALO, here, :]) + (cour[z, own, :] * lap + source)
                    nxt[z + HALO, here, :] = adv
                    g = adv * acc[t, z, own, :]
                    grad[xb, z] = g if t == 0 else grad[xb, z] + g
            return 0

        lax.fori_loop(0, rows // (TX * UNROLL), block, 0)

    def last_copy(j):
        part = pl.ds(slab(j), chunk)
        return pltpu.make_async_copy(
            buf[steps % 2].at[pl.ds(slab(j) + HALO, chunk), inner, :], last_hbm.at[0, part], fsem.at[j]
        )

    def send(j):
        part = pl.ds(slab(j), chunk)

        def pack(p, _):
            packed[j, p] = grad[inv_ref[p], part]
            return 0

        lax.fori_loop(0, places, pack, 0, unroll=4)
        for m in range(1, n_shot):
            data_copy(j, m).start()

    load(0, 0).wait()

    def sweep(i, _):
        for t in range(steps):
            j = i - t

            @pl.when((j >= 0) & (j < chunks))
            def _():
                if t == 0:
                    @pl.when(j + 1 < chunks)
                    def _():
                        load(0, j + 1).wait()

                    load(1, j).wait()
                    load(2, j).wait()
                load_acc(t, j).wait()

                @pl.when(j == 0)
                def _():
                    wait_halo(t, 0)

                @pl.when(j == chunks - 1)
                def _():
                    wait_halo(t, 1)

                advance(t, j)
                if t + 1 < steps:
                    @pl.when(j == 0)
                    def _():
                        start_halo(t + 1, 0)

                    @pl.when(j == chunks - 1)
                    def _():
                        start_halo(t + 1, 1)
                else:
                    send(j)
                    last_copy(j).start()

        return 0

    lax.fori_loop(0, chunks + steps - 1, sweep, 0)

    far = lax.broadcasted_iota(jnp.int32, taps.shape, 0).astype(jnp.float32)
    ratio = 2.0 * far / depth
    taps[...] = jnp.exp(-(ratio * ratio))
    row_i = lax.broadcasted_iota(jnp.int32, (depth, 3 * depth), 0)
    row_j = lax.broadcasted_iota(jnp.int32, (depth, 3 * depth), 1) - depth
    gap = row_i - row_j
    whole = row_j + sub * depth
    ratio = 2.0 * gap.astype(jnp.float32) / depth
    valid = (jnp.abs(gap) <= depth) & (whole >= 0) & (whole < n_sub * depth)
    total = jnp.sum(jnp.where(valid, jnp.exp(-(ratio * ratio)), 0.0), axis=1, keepdims=True)
    scale[...] = jnp.broadcast_to(1.0 / total, scale.shape)
    smooth[...] = jnp.zeros(smooth.shape, jnp.float32)

    def spread(first, low, high):
        def row(i, _):
            w = []
            for k in range(chunk):
                gap = i - (first + k - depth)
                away = jnp.maximum(gap, -gap)
                w.append(jnp.where(away <= depth, taps[jnp.minimum(away, depth)], 0.0))
            for g in range(TILES_OWN):
                s = smooth[g, i]
                for k in range(chunk):
                    s = s + w[k] * tiles[first + k, g]
                smooth[g, i] = s
            return 0

        lax.fori_loop(low, high, row, 0)

    def collect(j):
        z0 = slab(j)

        def tile(g, _):
            sums = [None] * chunk
            for p in range(places):
                if p < CAP:
                    hit = ids_ref[CAP * shot + p] == g
                    block = [packed[j, CAP * shot + p, k] for k in range(chunk)]
                else:
                    hit = rids[p] == g
                    block = [recv[j, p, k] for k in range(chunk)]
                for k in range(chunk):
                    term = jnp.where(hit, block[k], 0.0)
                    sums[k] = term if sums[k] is None else sums[k] + term
            for k in range(chunk):
                tiles[depth + z0 + k, g] = sums[k]
            return 0

        lax.fori_loop(0, TILES_OWN, tile, 0)

    def pass_on(j, side):
        z0 = slab(j)
        land, device = (2 * depth + z0, sub - 1) if side == 0 else (z0, sub + 1)
        return pltpu.make_async_remote_copy(
            src_ref=tiles.at[pl.ds(depth + z0, chunk)], dst_ref=tiles.at[pl.ds(land, chunk)],
            send_sem=nsend.at[j, side], recv_sem=nrecv.at[j, side],
            device_id={"sub": device}, device_id_type=MESH,
        )

    def finish(j):
        z0 = chunk * (chunks - 1) - slab(j)

        @pl.when(has_low)
        def _():
            pass_on(j, 0).wait_send()
            pass_on(j, 1).wait_recv()
            spread(z0, 0, z0 + chunk)

        @pl.when(has_high)
        def _():
            pass_on(j, 1).wait_send()
            pass_on(j, 0).wait_recv()
            spread(2 * depth + z0, z0, depth)

    for m in range(1, n_shot):
        ids_copy(m).wait()

    def gather(j, _):
        for m in range(1, n_shot):
            data_copy(j, m).wait()
        collect(j)

        @pl.when(has_low)
        def _():
            pass_on(j, 0).start()

        @pl.when(has_high)
        def _():
            pass_on(j, 1).start()

        spread(depth + slab(j), 0, depth)

        @pl.when(j > 0)
        def _():
            finish(j - 1)

        return 0

    lax.fori_loop(0, chunks, gather, 0)
    finish(chunks - 1)

    def normal(i, _):
        s = scale[pl.ds(i, TX, stride=0), :]
        for g in range(TILES_OWN):
            smooth[g, i] = smooth[g, i] * s
        return 0

    lax.fori_loop(0, depth, normal, 0)
    done = pltpu.make_async_copy(smooth, out_hbm, osem)
    done.start()
    for j in range(chunks):
        last_copy(j).wait()
    done.wait()


def body(courant, adjoint_prev, adjoint_now, forward_accel, traces, receivers, owners, tile_slot):
    n_sub = lax.axis_size("sub")
    n_shot = lax.axis_size("shot")
    _, steps, depth, rows, cols = forward_accel.shape
    places = n_shot * CAP
    chunks = depth // HALO
    f32 = jnp.float32
    smem = pl.BlockSpec(memory_space=pltpu.SMEM)
    vmem = pl.BlockSpec(memory_space=pltpu.VMEM)
    hbm = pl.BlockSpec(memory_space=pl.ANY)

    source, inverse, ids = pl.pallas_call(
        functools.partial(prepare_kernel, depth * rows * cols, cols),
        out_shape=(
            jax.ShapeDtypeStruct(((depth * rows + 2) * steps, cols), f32),
            jax.ShapeDtypeStruct((places,), jnp.int32),
            jax.ShapeDtypeStruct((places, TX, cols), jnp.int32),
        ),
        in_specs=[smem, vmem, smem, smem],
        out_specs=(vmem, smem, vmem),
        scratch_shapes=[pltpu.SMEM((n_shot,), jnp.int32)],
        compiler_params=pltpu.CompilerParams(vmem_limit_bytes=32 * 2**20),
        name="prepare",
    )(receivers, traces, owners.reshape(-1), tile_slot.reshape(-1))

    last, smoothed = pl.pallas_call(
        functools.partial(adjoint_kernel, n_shot, n_sub),
        out_shape=(
            jax.ShapeDtypeStruct((1, depth, rows, cols), f32),
            jax.ShapeDtypeStruct((TILES_OWN, depth, TX, cols), f32),
        ),
        in_specs=[smem, vmem, vmem] + [hbm] * 4,
        out_specs=(hbm, hbm),
        scratch_shapes=[
            pltpu.VMEM((depth + 2 * HALO, rows + 2 * PAD, cols), f32),
            pltpu.VMEM((depth + 2 * HALO, rows + 2 * PAD, cols), f32),
            pltpu.VMEM((depth, rows, cols), f32),
            pltpu.VMEM((steps, depth, rows, cols), f32),
            pltpu.VMEM((rows // TX, depth, TX, cols), f32),
            pltpu.VMEM((chunks, places, HALO, TX, cols), f32),
            pltpu.VMEM((chunks, places, HALO, TX, cols), f32),
            pltpu.VMEM((places, TX, cols), jnp.int32),
            pltpu.VMEM((3 * depth, TILES_OWN, TX, cols), f32),
            pltpu.VMEM((TILES_OWN, depth, TX, cols), f32),
            pltpu.VMEM((depth + 1, TX, cols), f32),
            pltpu.VMEM((depth, cols), f32),
            pltpu.SemaphoreType.DMA((3, chunks)),
            pltpu.SemaphoreType.DMA((steps, chunks)),
            pltpu.SemaphoreType.DMA((steps, 2)),
            pltpu.SemaphoreType.DMA((steps, 2)),
            pltpu.SemaphoreType.DMA((n_shot,)),
            pltpu.SemaphoreType.DMA((n_shot,)),
            pltpu.SemaphoreType.DMA((chunks, n_shot)),
            pltpu.SemaphoreType.DMA((chunks, n_shot)),
            pltpu.SemaphoreType.DMA((chunks, 2)),
            pltpu.SemaphoreType.DMA((chunks, 2)),
            pltpu.SemaphoreType.DMA((chunks,)),
            pltpu.SemaphoreType.DMA,
        ],
        compiler_params=pltpu.CompilerParams(
            collective_id=0, has_side_effects=True, vmem_limit_bytes=40 * 2**20
        ),
        name="adjoint",
    )(inverse, ids, source, courant, adjoint_prev, adjoint_now, forward_accel)
    return (smoothed, last)


def solution(mesh):
    placed = (
        P("shot", "sub", None, None),
        P("shot", "sub", None, None),
        P("shot", "sub", None, None),
        P("shot", None, "sub", None, None),
        P("shot", None, None),
        P("shot", None),
        P("shot", "sub", None, None),
        P("shot", "sub", None),
    )
    return jax.shard_map(
        body,
        mesh=mesh,
        in_specs=placed,
        out_specs=(P("shot", "sub", None, None), P("shot", "sub", None, None)),
        check_vma=False,
    )
```

```python
import functools

import jax
import jax.numpy as jnp
from jax import lax
from jax.experimental import pallas as pl
from jax.experimental.pallas import tpu as pltpu
from jax.sharding import PartitionSpec as P

TX = 8
TILES_OWN = 8
CAP = 2
HALO = 4
PAD = 8
UNROLL = 4
MESH = pl.DeviceIdType.MESH

stencil_weights = (-205.0 / 72.0, 8.0 / 5.0, -1.0 / 5.0, 8.0 / 315.0, -1.0 / 560.0)


def prepare_kernel(
    slab_cells, cols_y, rec_hbm, tr_hbm, own_hbm, slot_hbm, src_ref, inv_ref, ids_ref,
    count_ref, rec_ref, tr_ref, own_ref, slot_ref, sems,
):
    arrivals = [
        pltpu.make_async_copy(a, b, sems.at[i])
        for i, (a, b) in enumerate(
            ((rec_hbm, rec_ref), (tr_hbm, tr_ref), (own_hbm, own_ref), (slot_hbm, slot_ref))
        )
    ]
    for c in arrivals:
        c.start()
    steps = tr_ref.shape[1]
    spare = slab_cells // cols_y
    zrows = 256

    def zero(i, _):
        src_ref[pl.ds(pl.multiple_of(i * zrows, zrows), zrows), :] = jnp.zeros((zrows, cols_y), jnp.float32)
        return 0

    lax.fori_loop(0, spare * steps // zrows, zero, 0)
    ids_ref[...] = jnp.full(ids_ref.shape, -1, jnp.int32)
    for c in arrivals:
        c.wait()
    base = lax.axis_index("sub") * slab_cells
    lane = lax.broadcasted_iota(jnp.int32, (steps, cols_y), 1)
    group = 128

    def add(g, _):
        first = pl.multiple_of(g * group, group)
        values = tr_ref[0, :, pl.ds(first, group)]
        for r in range(group):
            off = rec_ref[0, first + r] - base
            inside = (off >= 0) & (off < slab_cells)
            row = jnp.where(inside, lax.div(off, cols_y), spare)
            at = pl.ds(pl.multiple_of(row * steps, steps), steps)
            value = jnp.broadcast_to(values[:, r : r + 1], (steps, cols_y))
            src_ref[at, :] += jnp.where(lane == lax.rem(off, cols_y), value, 0.0)
        return 0

    lax.fori_loop(0, rec_ref.shape[1] // group, add, 0)

    for i in range(count_ref.shape[0]):
        count_ref[i] = 0
    for i in range(inv_ref.shape[0]):
        inv_ref[i] = 0
    for k in range(slot_ref.shape[0]):
        owner = own_ref[k]
        place = owner * CAP + count_ref[owner]
        count_ref[owner] = count_ref[owner] + 1
        inv_ref[place] = k
        ids_ref[pl.ds(place, 1)] = jnp.full((1,) + ids_ref.shape[1:], slot_ref[k], jnp.int32)


def adjoint_kernel(
    n_shot, n_sub, inv_ref, ids_ref, src_ref, cour_hbm, prev_hbm, now_hbm, acc_hbm,
    last, smooth,
    even, odd, cour, acc, grad, packed, recv, rids, tiles, taps, scale,
    lsem, asem, hsend, hrecv, isend, irecv, dsend, drecv, nsend, nrecv,
):
    buf = (even, odd)
    shot, sub = lax.axis_index("shot"), lax.axis_index("sub")
    steps, depth, rows, cols = acc.shape
    places = packed.shape[1]
    chunk = HALO
    chunks = depth // chunk
    inner = pl.ds(PAD, rows)
    rising = lax.rem(sub, 2)
    front, back = sub + 1 - 2 * rising, sub - 1 + 2 * rising
    has_front = (front >= 0) & (front < n_sub)
    has_back = (back >= 0) & (back < n_sub)
    has_low, has_high = sub > 0, sub < n_sub - 1

    def slab(j):
        return chunk * (rising * j + (1 - rising) * (chunks - 1 - j))

    def load(which, j):
        part = pl.ds(slab(j), chunk)
        inside = pl.ds(slab(j) + HALO, chunk)
        if which == 0:
            return pltpu.make_async_copy(now_hbm.at[0, part], even.at[inside, inner, :], lsem.at[0, j])
        if which == 1:
            return pltpu.make_async_copy(prev_hbm.at[0, part], odd.at[inside, inner, :], lsem.at[1, j])
        return pltpu.make_async_copy(cour_hbm.at[0, part], cour.at[part], lsem.at[2, j])

    def load_acc(t, j):
        part = pl.ds(slab(j), chunk)
        return pltpu.make_async_copy(acc_hbm.at[0, t, part], acc.at[t, part], asem.at[t, j])

    load(0, 0).start()
    for i in range(chunks + steps - 1):
        for t in range(steps):
            j = i - t
            if 0 <= j < chunks:
                if t == 0:
                    if j + 1 < chunks:
                        load(0, j + 1).start()
                    load(1, j).start()
                    load(2, j).start()
                load_acc(t, j).start()

    barrier = pltpu.get_barrier_semaphore()

    def peer_of(m):
        return lax.rem(shot + m, n_shot)

    for m in range(1, n_shot):
        pl.semaphore_signal(barrier, inc=1, device_id={"shot": peer_of(m)}, device_id_type=MESH)

    @pl.when(has_front)
    def _():
        pl.semaphore_signal(barrier, inc=1, device_id={"sub": front}, device_id_type=MESH)

    @pl.when(has_back)
    def _():
        pl.semaphore_signal(barrier, inc=1, device_id={"sub": back}, device_id_type=MESH)

    for ref in buf:
        for rim in (0, PAD + rows):
            ref[HALO : HALO + depth, rim : rim + PAD, :] = jnp.zeros((depth, PAD, cols), jnp.float32)

    def clear(first):
        for ref in buf:
            ref[first : first + HALO, inner, :] = jnp.zeros((HALO, rows, cols), jnp.float32)

    @pl.when(jnp.logical_not(has_low))
    def _():
        clear(0)

    @pl.when(jnp.logical_not(has_high))
    def _():
        clear(HALO + depth)

    near = jnp.minimum(sub, 1) + jnp.minimum(n_sub - 1 - sub, 1)
    pl.semaphore_wait(barrier, n_shot - 1 + near)

    def halo(t, side):
        b = buf[t % 2]
        if side == 0:
            first, land, device = (1 - rising) * (depth - HALO), rising * (depth + HALO), front
        else:
            first, land, device = rising * (depth - HALO), (1 - rising) * (depth + HALO), back
        source = now_hbm.at[0, pl.ds(first, HALO)] if t == 0 else b.at[pl.ds(first + HALO, HALO), inner, :]
        return pltpu.make_async_remote_copy(
            src_ref=source, dst_ref=b.at[pl.ds(land, HALO), inner, :],
            send_sem=hsend.at[t, side], recv_sem=hrecv.at[t, side],
            device_id={"sub": device}, device_id_type=MESH,
        )

    there = (has_front, has_back)

    def start_halo(t, side):
        @pl.when(there[side])
        def _():
            halo(t, side).start()

    def wait_halo(t, side):
        @pl.when(there[side])
        def _():
            halo(t, side).wait()

    start_halo(0, 0)
    start_halo(0, 1)

    def ids_copy(m):
        peer = peer_of(m)
        return pltpu.make_async_remote_copy(
            src_ref=ids_ref.at[pl.ds(CAP * peer, CAP)], dst_ref=rids.at[pl.ds(CAP * m, CAP)],
            send_sem=isend.at[m], recv_sem=irecv.at[m],
            device_id={"shot": peer}, device_id_type=MESH,
        )

    def data_copy(j, m):
        peer = peer_of(m)
        return pltpu.make_async_remote_copy(
            src_ref=packed.at[j, pl.ds(CAP * peer, CAP)], dst_ref=recv.at[j, pl.ds(CAP * m, CAP)],
            send_sem=dsend.at[j, m], recv_sem=drecv.at[j, m],
            device_id={"shot": peer}, device_id_type=MESH,
        )

    for m in range(1, n_shot):
        ids_copy(m).start()

    lane = lax.broadcasted_iota(jnp.int32, (TX, cols), 1)
    from_left = [None] + [jnp.where(lane >= d, stencil_weights[d], 0.0) for d in range(1, 5)]
    from_right = [None] + [jnp.where(lane < cols - d, stencil_weights[d], 0.0) for d in range(1, 5)]

    def advance(t, j):
        cur, nxt = buf[t % 2], buf[(t + 1) % 2]
        z0 = slab(j)

        def block(i, _):
            for u in range(UNROLL):
                xb = i * UNROLL + u
                x0 = pl.multiple_of(xb * TX, TX)
                own = pl.ds(x0, TX)
                here = pl.ds(pl.multiple_of(x0 + PAD, TX), TX)
                col = {k: cur[z0 + (k + HALO), here, :] for k in range(-HALO, chunk + HALO)}
                for k in range(chunk):
                    z = z0 + k
                    c = col[k]
                    lap = (3.0 * stencil_weights[0]) * c
                    for d in range(1, 5):
                        pair = (col[k + d] + col[k - d]) + (
                            cur[z + HALO, pl.ds(x0 + (PAD + d), TX), :]
                            + cur[z + HALO, pl.ds(x0 + (PAD - d), TX), :]
                        )
                        lap = lap + stencil_weights[d] * pair
                        lap = lap + from_left[d] * pltpu.roll(c, d, 1)
                        lap = lap + from_right[d] * pltpu.roll(c, cols - d, 1)
                    source = src_ref[pl.ds((z * rows + x0) * steps + t, TX, stride=steps), :]
                    adv = (2.0 * c - nxt[z + HALO, here, :]) + (cour[z, own, :] * lap + source)
                    if t + 1 < steps:
                        nxt[z + HALO, here, :] = adv
                    else:
                        last[0, z, own, :] = adv
                    g = adv * acc[t, z, own, :]
                    grad[xb, z] = g if t == 0 else grad[xb, z] + g
            return 0

        lax.fori_loop(0, rows // (TX * UNROLL), block, 0)

    def send(j):
        part = pl.ds(slab(j), chunk)

        def pack(p, _):
            packed[j, p] = grad[inv_ref[p], part]
            return 0

        lax.fori_loop(0, places, pack, 0, unroll=4)
        for m in range(1, n_shot):
            data_copy(j, m).start()

    load(0, 0).wait()

    def sweep(i, _):
        for t in range(steps):
            j = i - t

            @pl.when((j >= 0) & (j < chunks))
            def _():
                if t == 0:
                    @pl.when(j + 1 < chunks)
                    def _():
                        load(0, j + 1).wait()

                    load(1, j).wait()
                    load(2, j).wait()
                load_acc(t, j).wait()

                @pl.when(j == 0)
                def _():
                    wait_halo(t, 0)

                @pl.when(j == chunks - 1)
                def _():
                    wait_halo(t, 1)

                advance(t, j)
                if t + 1 < steps:
                    @pl.when(j == 0)
                    def _():
                        start_halo(t + 1, 0)

                    @pl.when(j == chunks - 1)
                    def _():
                        start_halo(t + 1, 1)
                else:
                    send(j)

        return 0

    lax.fori_loop(0, chunks + steps - 1, sweep, 0)

    far = lax.broadcasted_iota(jnp.int32, taps.shape, 0).astype(jnp.float32)
    ratio = 2.0 * far / depth
    taps[...] = jnp.exp(-(ratio * ratio))
    row_i = lax.broadcasted_iota(jnp.int32, (depth, 3 * depth), 0)
    row_j = lax.broadcasted_iota(jnp.int32, (depth, 3 * depth), 1) - depth
    gap = row_i - row_j
    whole = row_j + sub * depth
    ratio = 2.0 * gap.astype(jnp.float32) / depth
    valid = (jnp.abs(gap) <= depth) & (whole >= 0) & (whole < n_sub * depth)
    total = jnp.sum(jnp.where(valid, jnp.exp(-(ratio * ratio)), 0.0), axis=1, keepdims=True)
    scale[...] = jnp.broadcast_to(1.0 / total, scale.shape)
    smooth[...] = jnp.zeros(smooth.shape, jnp.float32)

    def spread(first, low, high):
        def row(i, _):
            w = []
            for k in range(chunk):
                gap = i - (first + k - depth)
                away = jnp.maximum(gap, -gap)
                w.append(jnp.where(away <= depth, taps[jnp.minimum(away, depth)], 0.0))
            for g in range(TILES_OWN):
                s = smooth[g, i]
                for k in range(chunk):
                    s = s + w[k] * tiles[first + k, g]
                smooth[g, i] = s
            return 0

        lax.fori_loop(low, high, row, 0)

    def collect(j):
        z0 = slab(j)

        def tile(g, _):
            sums = [None] * chunk
            for p in range(places):
                if p < CAP:
                    hit = ids_ref[CAP * shot + p] == g
                    block = [packed[j, CAP * shot + p, k] for k in range(chunk)]
                else:
                    hit = rids[p] == g
                    block = [recv[j, p, k] for k in range(chunk)]
                for k in range(chunk):
                    term = jnp.where(hit, block[k], 0.0)
                    sums[k] = term if sums[k] is None else sums[k] + term
            for k in range(chunk):
                tiles[depth + z0 + k, g] = sums[k]
            return 0

        lax.fori_loop(0, TILES_OWN, tile, 0)

    def pass_on(j, side):
        z0 = slab(j)
        land, device = (2 * depth + z0, sub - 1) if side == 0 else (z0, sub + 1)
        return pltpu.make_async_remote_copy(
            src_ref=tiles.at[pl.ds(depth + z0, chunk)], dst_ref=tiles.at[pl.ds(land, chunk)],
            send_sem=nsend.at[j, side], recv_sem=nrecv.at[j, side],
            device_id={"sub": device}, device_id_type=MESH,
        )

    def finish(j):
        z0 = chunk * (chunks - 1) - slab(j)

        @pl.when(has_low)
        def _():
            pass_on(j, 0).wait_send()
            pass_on(j, 1).wait_recv()
            spread(z0, 0, z0 + chunk)

        @pl.when(has_high)
        def _():
            pass_on(j, 1).wait_send()
            pass_on(j, 0).wait_recv()
            spread(2 * depth + z0, z0, depth)

    for m in range(1, n_shot):
        ids_copy(m).wait()

    def gather(j, _):
        for m in range(1, n_shot):
            data_copy(j, m).wait()
        collect(j)

        @pl.when(has_low)
        def _():
            pass_on(j, 0).start()

        @pl.when(has_high)
        def _():
            pass_on(j, 1).start()

        spread(depth + slab(j), 0, depth)

        @pl.when(j > 0)
        def _():
            finish(j - 1)

        return 0

    lax.fori_loop(0, chunks, gather, 0)
    finish(chunks - 1)

    def normal(i, _):
        s = scale[pl.ds(i, TX, stride=0), :]
        for g in range(TILES_OWN):
            smooth[g, i] = smooth[g, i] * s
        return 0

    lax.fori_loop(0, depth, normal, 0)


def store_kernel(smooth_ref, last_ref, smooth_hbm, last_hbm, sems):
    copies = [
        pltpu.make_async_copy(last_ref, last_hbm, sems.at[0]),
        pltpu.make_async_copy(smooth_ref, smooth_hbm, sems.at[1]),
    ]
    for c in copies:
        c.start()
    for c in copies:
        c.wait()


def body(courant, adjoint_prev, adjoint_now, forward_accel, traces, receivers, owners, tile_slot):
    n_sub = lax.axis_size("sub")
    n_shot = lax.axis_size("shot")
    _, steps, depth, rows, cols = forward_accel.shape
    places = n_shot * CAP
    chunks = depth // HALO
    f32 = jnp.float32
    smem = pl.BlockSpec(memory_space=pltpu.SMEM)
    vmem = pl.BlockSpec(memory_space=pltpu.VMEM)
    hbm = pl.BlockSpec(memory_space=pl.ANY)

    def in_hbm(x):
        return pltpu.with_memory_space_constraint(x, pltpu.HBM)

    def in_vmem(x):
        return pltpu.with_memory_space_constraint(x, pltpu.VMEM)

    source, inverse, ids = pl.pallas_call(
        functools.partial(prepare_kernel, depth * rows * cols, cols),
        out_shape=(
            pltpu.VMEM(((depth * rows + 2) * steps, cols), f32),
            jax.ShapeDtypeStruct((places,), jnp.int32),
            pltpu.VMEM((places, TX, cols), jnp.int32),
        ),
        in_specs=[hbm] * 4,
        out_specs=(vmem, smem, vmem),
        scratch_shapes=[
            pltpu.SMEM((n_shot,), jnp.int32),
            pltpu.SMEM(receivers.shape, jnp.int32),
            pltpu.VMEM(traces.shape, f32),
            pltpu.SMEM((owners.size,), jnp.int32),
            pltpu.SMEM((tile_slot.size,), jnp.int32),
            pltpu.SemaphoreType.DMA((4,)),
        ],
        compiler_params=pltpu.CompilerParams(vmem_limit_bytes=32 * 2**20),
        name="prepare",
    )(*(in_hbm(x) for x in (receivers, traces, owners.reshape(-1), tile_slot.reshape(-1))))

    last, smoothed = pl.pallas_call(
        functools.partial(adjoint_kernel, n_shot, n_sub),
        out_shape=(
            pltpu.VMEM((1, depth, rows, cols), f32),
            pltpu.VMEM((TILES_OWN, depth, TX, cols), f32),
        ),
        in_specs=[smem, vmem, vmem] + [hbm] * 4,
        out_specs=(vmem, vmem),
        scratch_shapes=[
            pltpu.VMEM((depth + 2 * HALO, rows + 2 * PAD, cols), f32),
            pltpu.VMEM((depth + 2 * HALO, rows + 2 * PAD, cols), f32),
            pltpu.VMEM((depth, rows, cols), f32),
            pltpu.VMEM((steps, depth, rows, cols), f32),
            pltpu.VMEM((rows // TX, depth, TX, cols), f32),
            pltpu.VMEM((chunks, places, HALO, TX, cols), f32),
            pltpu.VMEM((chunks, places, HALO, TX, cols), f32),
            pltpu.VMEM((places, TX, cols), jnp.int32),
            pltpu.VMEM((3 * depth, TILES_OWN, TX, cols), f32),
            pltpu.VMEM((depth + 1, TX, cols), f32),
            pltpu.VMEM((depth, cols), f32),
            pltpu.SemaphoreType.DMA((3, chunks)),
            pltpu.SemaphoreType.DMA((steps, chunks)),
            pltpu.SemaphoreType.DMA((steps, 2)),
            pltpu.SemaphoreType.DMA((steps, 2)),
            pltpu.SemaphoreType.DMA((n_shot,)),
            pltpu.SemaphoreType.DMA((n_shot,)),
            pltpu.SemaphoreType.DMA((chunks, n_shot)),
            pltpu.SemaphoreType.DMA((chunks, n_shot)),
            pltpu.SemaphoreType.DMA((chunks, 2)),
            pltpu.SemaphoreType.DMA((chunks, 2)),
        ],
        compiler_params=pltpu.CompilerParams(
            collective_id=0, has_side_effects=True, vmem_limit_bytes=40 * 2**20
        ),
        name="adjoint",
    )(
        inverse, in_vmem(ids), in_vmem(source),
        *(in_hbm(x) for x in (courant, adjoint_prev, adjoint_now, forward_accel)),
    )

    smoothed, last = pl.pallas_call(
        store_kernel,
        out_shape=tuple(pltpu.HBM(x.shape, f32) for x in (smoothed, last)),
        in_specs=[hbm, hbm],
        out_specs=(hbm, hbm),
        scratch_shapes=[pltpu.SemaphoreType.DMA((2,))],
        name="store",
    )(in_vmem(smoothed), in_vmem(last))
    return (smoothed, last)


def solution(mesh):
    placed = (
        P("shot", "sub", None, None),
        P("shot", "sub", None, None),
        P("shot", "sub", None, None),
        P("shot", None, "sub", None, None),
        P("shot", None, None),
        P("shot", None),
        P("shot", "sub", None, None),
        P("shot", "sub", None),
    )
    return jax.shard_map(
        body,
        mesh=mesh,
        in_specs=placed,
        out_specs=(P("shot", "sub", None, None), P("shot", "sub", None, None)),
        check_vma=False,
    )
```

```python
import functools

import jax
import jax.numpy as jnp
from jax import lax
from jax.experimental import pallas as pl
from jax.experimental.pallas import tpu as pltpu
from jax.sharding import PartitionSpec as P

TX = 8
TILES_OWN = 8
CAP = 2
HALO = 4
PAD = 8
UNROLL = 8
MESH = pl.DeviceIdType.MESH

stencil_weights = (-205.0 / 72.0, 8.0 / 5.0, -1.0 / 5.0, 8.0 / 315.0, -1.0 / 560.0)


def prepare_kernel(
    slab_cells, cols_y, rec_hbm, tr_hbm, own_hbm, slot_hbm, src_ref, inv_ref, ids_ref,
    count_ref, rec_ref, tr_ref, own_ref, slot_ref, sems,
):
    arrivals = [
        pltpu.make_async_copy(a, b, sems.at[i])
        for i, (a, b) in enumerate(
            ((rec_hbm, rec_ref), (tr_hbm, tr_ref), (own_hbm, own_ref), (slot_hbm, slot_ref))
        )
    ]
    for c in arrivals:
        c.start()
    steps = tr_ref.shape[1]
    spare = slab_cells // cols_y
    shift = cols_y.bit_length() - 1
    assert cols_y == 1 << shift
    zrows = 256

    def zero(i, _):
        src_ref[pl.ds(pl.multiple_of(i * zrows, zrows), zrows), :] = jnp.zeros((zrows, cols_y), jnp.float32)
        return 0

    lax.fori_loop(0, spare * steps // zrows, zero, 0)
    ids_ref[...] = jnp.full(ids_ref.shape, -1, jnp.int32)
    for c in arrivals:
        c.wait()
    base = lax.axis_index("sub") * slab_cells
    lane = lax.broadcasted_iota(jnp.int32, (steps, cols_y), 1)
    group = 128

    def add(g, _):
        first = pl.multiple_of(g * group, group)
        values = tr_ref[0, :, pl.ds(first, group)]
        for r in range(group):
            off = rec_ref[0, first + r] - base
            row = jnp.right_shift(off, shift)
            row = jnp.minimum(row.astype(jnp.uint32), jnp.uint32(spare)).astype(jnp.int32)
            at = pl.ds(pl.multiple_of(row * steps, steps), steps)
            value = jnp.broadcast_to(values[:, r : r + 1], (steps, cols_y))
            src_ref[at, :] += jnp.where(lane == jnp.bitwise_and(off, cols_y - 1), value, 0.0)
        return 0

    lax.fori_loop(0, rec_ref.shape[1] // group, add, 0)

    for i in range(count_ref.shape[0]):
        count_ref[i] = 0
    for i in range(inv_ref.shape[0]):
        inv_ref[i] = 0
    for k in range(slot_ref.shape[0]):
        owner = own_ref[k]
        place = owner * CAP + count_ref[owner]
        count_ref[owner] = count_ref[owner] + 1
        inv_ref[place] = k
        ids_ref[pl.ds(place, 1)] = jnp.full((1,) + ids_ref.shape[1:], slot_ref[k], jnp.int32)


def adjoint_kernel(
    n_shot, n_sub, inv_ref, ids_ref, src_ref, cour_hbm, prev_hbm, now_hbm, acc_hbm,
    last, smooth,
    even, odd, cour, acc, grad, packed, recv, rids, tiles, taps, scale, along,
    lsem, hsend, hrecv, isend, irecv, dsend, drecv, nsend, nrecv,
):
    buf = (even, odd)
    shot, sub = lax.axis_index("shot"), lax.axis_index("sub")
    steps, depth, rows, cols = acc.shape
    places = packed.shape[1]
    chunk = HALO
    chunks = depth // chunk
    inner = pl.ds(PAD, rows)
    rising = lax.rem(sub, 2)
    front, back = sub + 1 - 2 * rising, sub - 1 + 2 * rising
    has_front = (front >= 0) & (front < n_sub)
    has_back = (back >= 0) & (back < n_sub)
    has_low, has_high = sub > 0, sub < n_sub - 1

    def slab(j):
        return chunk * (rising * j + (1 - rising) * (chunks - 1 - j))

    barrier = pltpu.get_barrier_semaphore()

    def peer_of(m):
        return lax.rem(shot + m, n_shot)

    for m in range(1, n_shot):
        pl.semaphore_signal(barrier, inc=1, device_id={"shot": peer_of(m)}, device_id_type=MESH)

    @pl.when(has_front)
    def _():
        pl.semaphore_signal(barrier, inc=1, device_id={"sub": front}, device_id_type=MESH)

    @pl.when(has_back)
    def _():
        pl.semaphore_signal(barrier, inc=1, device_id={"sub": back}, device_id_type=MESH)

    def load(which, j):
        part = pl.ds(slab(j), chunk)
        inside = pl.ds(slab(j) + HALO, chunk)
        if which == 0:
            return pltpu.make_async_copy(now_hbm.at[0, part], even.at[inside, inner, :], lsem.at[0, j])
        if which == 1:
            return pltpu.make_async_copy(prev_hbm.at[0, part], odd.at[inside, inner, :], lsem.at[1, j])
        if which == 2:
            return pltpu.make_async_copy(cour_hbm.at[0, part], cour.at[part], lsem.at[2, j])
        return pltpu.make_async_copy(acc_hbm.at[0, :, part], acc.at[:, part], lsem.at[3, j])

    load(0, 0).start()
    load(0, 1).start()
    for j in (1, 0, *range(2, chunks)):
        if 0 < j < chunks - 1:
            load(0, j + 1).start()
        for which in (1, 2, 3):
            load(which, j).start()

    for ref in buf:
        for rim in (0, PAD + rows):
            ref[HALO : HALO + depth, rim : rim + PAD, :] = jnp.zeros((depth, PAD, cols), jnp.float32)

    def clear(first):
        for ref in buf:
            ref[first : first + HALO, inner, :] = jnp.zeros((HALO, rows, cols), jnp.float32)

    @pl.when(jnp.logical_not(has_low))
    def _():
        clear(0)

    @pl.when(jnp.logical_not(has_high))
    def _():
        clear(HALO + depth)

    near = jnp.minimum(sub, 1) + jnp.minimum(n_sub - 1 - sub, 1)
    pl.semaphore_wait(barrier, n_shot - 1 + near)

    def halo(t, side):
        b = buf[t % 2]
        if side == 0:
            first, land, device = (1 - rising) * (depth - HALO), rising * (depth + HALO), front
        else:
            first, land, device = rising * (depth - HALO), (1 - rising) * (depth + HALO), back
        source = now_hbm.at[0, pl.ds(first, HALO)] if t == 0 else b.at[pl.ds(first + HALO, HALO), inner, :]
        return pltpu.make_async_remote_copy(
            src_ref=source, dst_ref=b.at[pl.ds(land, HALO), inner, :],
            send_sem=hsend.at[t, side], recv_sem=hrecv.at[t, side],
            device_id={"sub": device}, device_id_type=MESH,
        )

    there = (has_front, has_back)

    def start_halo(t, side):
        @pl.when(there[side])
        def _():
            halo(t, side).start()

    def wait_halo(t, side):
        @pl.when(there[side])
        def _():
            halo(t, side).wait()

    start_halo(0, 0)
    start_halo(0, 1)

    def ids_copy(m):
        peer = peer_of(m)
        return pltpu.make_async_remote_copy(
            src_ref=ids_ref.at[pl.ds(CAP * peer, CAP)], dst_ref=rids.at[pl.ds(CAP * m, CAP)],
            send_sem=isend, recv_sem=irecv, device_id={"shot": peer}, device_id_type=MESH,
        )

    def data_copy(j, m):
        peer = peer_of(m)
        return pltpu.make_async_remote_copy(
            src_ref=packed.at[j, pl.ds(CAP * peer, CAP)], dst_ref=recv.at[j, pl.ds(CAP * m, CAP)],
            send_sem=dsend.at[j], recv_sem=drecv.at[j],
            device_id={"shot": peer}, device_id_type=MESH,
        )

    others = pl.ds(CAP, places - CAP)

    def ids_all():
        return pltpu.make_async_remote_copy(
            src_ref=ids_ref.at[others], dst_ref=rids.at[others],
            send_sem=isend, recv_sem=irecv, device_id={"shot": peer_of(1)}, device_id_type=MESH,
        )

    def data_all(j):
        return pltpu.make_async_remote_copy(
            src_ref=packed.at[j, others], dst_ref=recv.at[j, others],
            send_sem=dsend.at[j], recv_sem=drecv.at[j],
            device_id={"shot": peer_of(1)}, device_id_type=MESH,
        )

    for m in range(1, n_shot):
        ids_copy(m).start()

    across = lax.broadcasted_iota(jnp.int32, (cols, cols), 0) - lax.broadcasted_iota(jnp.int32, (cols, cols), 1)
    across = jnp.maximum(across, -across)
    matrix = jnp.where(across == 0, 3.0 * stencil_weights[0], 0.0)
    for d in range(1, 5):
        matrix = jnp.where(across == d, stencil_weights[d], matrix)
    coarse = matrix.astype(jnp.bfloat16)
    along[0:cols] = coarse
    along[cols : 2 * cols] = coarse
    along[2 * cols :] = (matrix - coarse.astype(jnp.float32)).astype(jnp.bfloat16)

    def advance(t, j):
        cur, nxt = buf[t % 2], buf[(t + 1) % 2]
        z0 = slab(j)

        def block(i, _):
            column = []
            for u in range(UNROLL):
                here = pl.ds(pl.multiple_of((i * UNROLL + u) * TX + PAD, TX), TX)
                column.append({k: cur[z0 + (k + HALO), here, :] for k in range(-HALO, chunk + HALO)})
            centre = jnp.concatenate([column[u][k] for u in range(UNROLL) for k in range(chunk)], axis=0)
            high = centre.astype(jnp.bfloat16)
            low = (centre - high.astype(jnp.float32)).astype(jnp.bfloat16)
            lap_y = jnp.dot(
                jnp.concatenate([high, low, high], axis=1), along[...], preferred_element_type=jnp.float32
            )
            for u in range(UNROLL):
                xb = i * UNROLL + u
                x0 = pl.multiple_of(xb * TX, TX)
                own = pl.ds(x0, TX)
                here = pl.ds(pl.multiple_of(x0 + PAD, TX), TX)
                col = column[u]
                for k in range(chunk):
                    z = z0 + k
                    c = col[k]
                    n = (u * chunk + k) * TX
                    lap = lap_y[n : n + TX]
                    for d in range(1, 5):
                        pair = (col[k + d] + col[k - d]) + (
                            cur[z + HALO, pl.ds(x0 + (PAD + d), TX), :]
                            + cur[z + HALO, pl.ds(x0 + (PAD - d), TX), :]
                        )
                        lap = lap + stencil_weights[d] * pair
                    source = src_ref[pl.ds((z * rows + x0) * steps + t, TX, stride=steps), :]
                    adv = (2.0 * c - nxt[z + HALO, here, :]) + (cour[z, own, :] * lap + source)
                    if t + 1 < steps:
                        nxt[z + HALO, here, :] = adv
                    else:
                        last[0, z, own, :] = adv
                    g = adv * acc[t, z, own, :]
                    grad[xb, z] = g if t == 0 else grad[xb, z] + g
            return 0

        lax.fori_loop(0, rows // (TX * UNROLL), block, 0)

    def send(j):
        part = pl.ds(slab(j), chunk)

        def pack(p, _):
            packed[j, p] = grad[inv_ref[p], part]
            return 0

        lax.fori_loop(0, places, pack, 0, unroll=4)
        for m in range(1, n_shot):
            data_copy(j, m).start()

    load(0, 0).wait()
    load(0, 1).wait()

    def step(t, j):
        if t == 0:
            @pl.when((j > 0) & (j < chunks - 1))
            def _():
                load(0, j + 1).wait()

            for which in (1, 2, 3):
                load(which, j).wait()

        @pl.when(j == 0)
        def _():
            wait_halo(t, 0)

        @pl.when(j == chunks - 1)
        def _():
            wait_halo(t, 1)

        advance(t, j)
        if t + 1 < steps:
            @pl.when(j == 0)
            def _():
                start_halo(t + 1, 0)

            @pl.when(j == chunks - 1)
            def _():
                start_halo(t + 1, 1)
        else:
            send(j)

    def sweep(i, _):
        many = jnp.where(i == 0, 2, jnp.where(i == 2, 0, jnp.where(i < chunks, 1, 0)))

        def initial(n, _):
            step(0, jnp.where(i == 0, 1 - n, jnp.where(i == 1, 2, i)))
            return 0

        lax.fori_loop(0, many, initial, 0)
        for t in range(1, steps):
            j = i - t

            @pl.when((j >= 0) & (j < chunks))
            def _():
                step(t, j)

        return 0

    lax.fori_loop(0, chunks + steps - 1, sweep, 0)

    far = lax.broadcasted_iota(jnp.int32, taps.shape, 0) - (2 * depth + chunk)
    ratio = 2.0 * far.astype(jnp.float32) / depth
    taps[...] = jnp.where(jnp.maximum(far, -far) <= depth, jnp.exp(-(ratio * ratio)), 0.0)
    row_i = lax.broadcasted_iota(jnp.int32, (depth, 3 * depth), 0)
    row_j = lax.broadcasted_iota(jnp.int32, (depth, 3 * depth), 1) - depth
    gap = row_i - row_j
    whole = row_j + sub * depth
    ratio = 2.0 * gap.astype(jnp.float32) / depth
    valid = (jnp.abs(gap) <= depth) & (whole >= 0) & (whole < n_sub * depth)
    total = jnp.sum(jnp.where(valid, jnp.exp(-(ratio * ratio)), 0.0), axis=1, keepdims=True)
    scale[...] = jnp.broadcast_to(1.0 / total, scale.shape)
    smooth[...] = jnp.zeros(smooth.shape, jnp.float32)

    def spread(first, low, high):
        def row(i, _):
            gap = i - (first - depth) + (2 * depth + chunk)
            w = [taps[gap - k] for k in range(chunk)]
            for g in range(TILES_OWN):
                s = w[0] * tiles[first, g] + w[1] * tiles[first + 1, g]
                for k in range(2, chunk, 2):
                    s = s + (w[k] * tiles[first + k, g] + w[k + 1] * tiles[first + k + 1, g])
                smooth[g, i] += s
            return 0

        lax.fori_loop(low, high, row, 0)

    def collect(j):
        z0 = slab(j)

        def tile(g, _):
            sums = [None] * chunk
            for p in range(places):
                if p < CAP:
                    hit = ids_ref[CAP * shot + p] == g
                    block = [packed[j, CAP * shot + p, k] for k in range(chunk)]
                else:
                    hit = rids[p] == g
                    block = [recv[j, p, k] for k in range(chunk)]
                for k in range(chunk):
                    term = jnp.where(hit, block[k], 0.0)
                    sums[k] = term if sums[k] is None else sums[k] + term
            for k in range(chunk):
                tiles[depth + z0 + k, g] = sums[k]
            return 0

        lax.fori_loop(0, TILES_OWN, tile, 0)

    def pass_on(j, side):
        z0 = slab(j)
        land, device = (2 * depth + z0, sub - 1) if side == 0 else (z0, sub + 1)
        return pltpu.make_async_remote_copy(
            src_ref=tiles.at[pl.ds(depth + z0, chunk)], dst_ref=tiles.at[pl.ds(land, chunk)],
            send_sem=nsend.at[j, side], recv_sem=nrecv.at[j, side],
            device_id={"sub": device}, device_id_type=MESH,
        )

    def finish(j):
        z0 = chunk * (chunks - 1) - slab(j)

        @pl.when(has_low)
        def _():
            pass_on(j, 0).wait_send()
            pass_on(j, 1).wait_recv()
            spread(z0, 0, z0 + chunk)

        @pl.when(has_high)
        def _():
            pass_on(j, 1).wait_send()
            pass_on(j, 0).wait_recv()
            spread(2 * depth + z0, z0, depth)

    ids_all().wait()

    def gather(j):
        data_all(j).wait()
        collect(j)

        @pl.when(has_low)
        def _():
            pass_on(j, 0).start()

        @pl.when(has_high)
        def _():
            pass_on(j, 1).start()

        spread(depth + slab(j), 0, depth)

    def gathers(j, _):
        gather(j)

        @pl.when(j > 0)
        def _():
            finish(j - 1)

        return 0

    lax.fori_loop(0, chunks - 1, gathers, 0)
    finish(chunks - 2)
    gather(chunks - 1)
    finish(chunks - 1)

    def normal(i, _):
        s = scale[pl.ds(i, TX, stride=0), :]
        for g in range(TILES_OWN):
            smooth[g, i] = smooth[g, i] * s
        return 0

    lax.fori_loop(0, depth, normal, 0)


def store_kernel(smooth_ref, last_ref, smooth_hbm, last_hbm, sems):
    copies = [
        pltpu.make_async_copy(last_ref, last_hbm, sems.at[0]),
        pltpu.make_async_copy(smooth_ref, smooth_hbm, sems.at[1]),
    ]
    for c in copies:
        c.start()
    for c in copies:
        c.wait()


def body(courant, adjoint_prev, adjoint_now, forward_accel, traces, receivers, owners, tile_slot):
    n_sub = lax.axis_size("sub")
    n_shot = lax.axis_size("shot")
    _, steps, depth, rows, cols = forward_accel.shape
    places = n_shot * CAP
    chunks = depth // HALO
    f32 = jnp.float32
    smem = pl.BlockSpec(memory_space=pltpu.SMEM)
    vmem = pl.BlockSpec(memory_space=pltpu.VMEM)
    hbm = pl.BlockSpec(memory_space=pl.ANY)

    def in_hbm(x):
        return pltpu.with_memory_space_constraint(x, pltpu.HBM)

    def in_vmem(x):
        return pltpu.with_memory_space_constraint(x, pltpu.VMEM)

    source, inverse, ids = pl.pallas_call(
        functools.partial(prepare_kernel, depth * rows * cols, cols),
        out_shape=(
            pltpu.VMEM(((depth * rows + 2) * steps, cols), f32),
            jax.ShapeDtypeStruct((places,), jnp.int32),
            pltpu.VMEM((places, TX, cols), jnp.int32),
        ),
        in_specs=[hbm] * 4,
        out_specs=(vmem, smem, vmem),
        scratch_shapes=[
            pltpu.SMEM((n_shot,), jnp.int32),
            pltpu.SMEM(receivers.shape, jnp.int32),
            pltpu.VMEM(traces.shape, f32),
            pltpu.SMEM((owners.size,), jnp.int32),
            pltpu.SMEM((tile_slot.size,), jnp.int32),
            pltpu.SemaphoreType.DMA((4,)),
        ],
        compiler_params=pltpu.CompilerParams(vmem_limit_bytes=32 * 2**20),
        name="prepare",
    )(*(in_hbm(x) for x in (receivers, traces, owners.reshape(-1), tile_slot.reshape(-1))))

    last, smoothed = pl.pallas_call(
        functools.partial(adjoint_kernel, n_shot, n_sub),
        out_shape=(
            pltpu.VMEM((1, depth, rows, cols), f32),
            pltpu.VMEM((TILES_OWN, depth, TX, cols), f32),
        ),
        in_specs=[smem, vmem, vmem] + [hbm] * 4,
        out_specs=(vmem, vmem),
        scratch_shapes=[
            pltpu.VMEM((depth + 2 * HALO, rows + 2 * PAD, cols), f32),
            pltpu.VMEM((depth + 2 * HALO, rows + 2 * PAD, cols), f32),
            pltpu.VMEM((depth, rows, cols), f32),
            pltpu.VMEM((steps, depth, rows, cols), f32),
            pltpu.VMEM((rows // TX, depth, TX, cols), f32),
            pltpu.VMEM((chunks, places, HALO, TX, cols), f32),
            pltpu.VMEM((chunks, places, HALO, TX, cols), f32),
            pltpu.VMEM((places, TX, cols), jnp.int32),
            pltpu.VMEM((3 * depth, TILES_OWN, TX, cols), f32),
            pltpu.VMEM((4 * depth + 2 * HALO, TX, cols), f32),
            pltpu.VMEM((depth, cols), f32),
            pltpu.VMEM((3 * cols, cols), jnp.bfloat16),
            pltpu.SemaphoreType.DMA((4, chunks)),
            pltpu.SemaphoreType.DMA((steps, 2)),
            pltpu.SemaphoreType.DMA((steps, 2)),
            pltpu.SemaphoreType.DMA,
            pltpu.SemaphoreType.DMA,
            pltpu.SemaphoreType.DMA((chunks,)),
            pltpu.SemaphoreType.DMA((chunks,)),
            pltpu.SemaphoreType.DMA((chunks, 2)),
            pltpu.SemaphoreType.DMA((chunks, 2)),
        ],
        compiler_params=pltpu.CompilerParams(
            collective_id=0, has_side_effects=True, vmem_limit_bytes=40 * 2**20
        ),
        name="adjoint",
    )(
        inverse, in_vmem(ids), in_vmem(source),
        *(in_hbm(x) for x in (courant, adjoint_prev, adjoint_now, forward_accel)),
    )

    smoothed, last = pl.pallas_call(
        store_kernel,
        out_shape=tuple(pltpu.HBM(x.shape, f32) for x in (smoothed, last)),
        in_specs=[hbm, hbm],
        out_specs=(hbm, hbm),
        scratch_shapes=[pltpu.SemaphoreType.DMA((2,))],
        name="store",
    )(in_vmem(smoothed), in_vmem(last))
    return (smoothed, last)


def solution(mesh):
    placed = (
        P("shot", "sub", None, None),
        P("shot", "sub", None, None),
        P("shot", "sub", None, None),
        P("shot", None, "sub", None, None),
        P("shot", None, None),
        P("shot", None),
        P("shot", "sub", None, None),
        P("shot", "sub", None),
    )
    return jax.shard_map(
        body,
        mesh=mesh,
        in_specs=placed,
        out_specs=(P("shot", "sub", None, None), P("shot", "sub", None, None)),
        check_vma=False,
    )
```

```python
import functools

import jax
import jax.numpy as jnp
from jax import lax
from jax.experimental import pallas as pl
from jax.experimental.pallas import tpu as pltpu
from jax.sharding import PartitionSpec as P

TX = 8
TILES_OWN = 8
CAP = 2
HALO = 4
PAD = 8
UNROLL = 8
MESH = pl.DeviceIdType.MESH

stencil_weights = (-205.0 / 72.0, 8.0 / 5.0, -1.0 / 5.0, 8.0 / 315.0, -1.0 / 560.0)


def prepare_kernel(
    slab_cells, cols_y, rec_hbm, tr_hbm, own_hbm, slot_hbm, src_ref, inv_ref, ids_ref,
    count_ref, rec_ref, tr_ref, own_ref, slot_ref, sems,
):
    arrivals = [
        pltpu.make_async_copy(a, b, sems.at[i])
        for i, (a, b) in enumerate(
            ((rec_hbm, rec_ref), (tr_hbm, tr_ref), (own_hbm, own_ref), (slot_hbm, slot_ref))
        )
    ]
    for c in arrivals:
        c.start()
    steps = tr_ref.shape[1]
    spare = slab_cells // cols_y
    shift = cols_y.bit_length() - 1
    assert cols_y == 1 << shift
    zrows = 256

    def zero(i, _):
        src_ref[pl.ds(pl.multiple_of(i * zrows, zrows), zrows), :] = jnp.zeros((zrows, cols_y), jnp.float32)
        return 0

    lax.fori_loop(0, spare * steps // zrows, zero, 0)
    ids_ref[...] = jnp.full(ids_ref.shape, -1, jnp.int32)
    for c in arrivals:
        c.wait()
    base = lax.axis_index("sub") * slab_cells
    lane = lax.broadcasted_iota(jnp.int32, (steps, cols_y), 1)
    group = 128

    def add(g, _):
        first = pl.multiple_of(g * group, group)
        values = tr_ref[0, :, pl.ds(first, group)]
        def place(r):
            off = rec_ref[0, first + r] - base
            row = jnp.right_shift(off, shift)
            row = jnp.minimum(row.astype(jnp.uint32), jnp.uint32(spare)).astype(jnp.int32)
            value = jnp.broadcast_to(values[:, r : r + 1], (steps, cols_y))
            value = jnp.where(lane == jnp.bitwise_and(off, cols_y - 1), value, 0.0)
            return row, pl.ds(pl.multiple_of(row * steps, steps), steps), value

        for r in range(0, group, 2):
            row_a, at_a, value_a = place(r)
            row_b, at_b, value_b = place(r + 1)
            old_a, old_b = src_ref[at_a, :], src_ref[at_b, :]
            both = jnp.where(row_a == row_b, value_a, 0.0)
            src_ref[at_a, :] = old_a + value_a
            src_ref[at_b, :] = old_b + (value_b + both)
        return 0

    lax.fori_loop(0, rec_ref.shape[1] // group, add, 0)

    for i in range(count_ref.shape[0]):
        count_ref[i] = 0
    for i in range(inv_ref.shape[0]):
        inv_ref[i] = 0
    for k in range(slot_ref.shape[0]):
        owner = own_ref[k]
        place = owner * CAP + count_ref[owner]
        count_ref[owner] = count_ref[owner] + 1
        inv_ref[place] = k
        ids_ref[pl.ds(place, 1)] = jnp.full((1,) + ids_ref.shape[1:], slot_ref[k], jnp.int32)


def adjoint_kernel(
    n_shot, n_sub, inv_ref, ids_ref, src_ref, cour_hbm, prev_hbm, now_hbm, acc_hbm,
    last, smooth,
    even, odd, cour, acc, grad, packed, recv, rids, tiles, taps, scale, along,
    lsem, hsend, hrecv, isend, irecv, dsend, drecv, nsend, nrecv,
):
    buf = (even, odd)
    shot, sub = lax.axis_index("shot"), lax.axis_index("sub")
    steps, depth, rows, cols = acc.shape
    places = packed.shape[1]
    chunk = HALO
    chunks = depth // chunk
    inner = pl.ds(PAD, rows)
    rising = lax.rem(sub, 2)
    front, back = sub + 1 - 2 * rising, sub - 1 + 2 * rising
    has_front = (front >= 0) & (front < n_sub)
    has_back = (back >= 0) & (back < n_sub)
    has_low, has_high = sub > 0, sub < n_sub - 1

    def slab(j):
        return chunk * (rising * j + (1 - rising) * (chunks - 1 - j))

    barrier = pltpu.get_barrier_semaphore()

    def peer_of(m):
        return lax.rem(shot + m, n_shot)

    for m in range(1, n_shot):
        pl.semaphore_signal(barrier, inc=1, device_id={"shot": peer_of(m)}, device_id_type=MESH)

    @pl.when(has_front)
    def _():
        pl.semaphore_signal(barrier, inc=1, device_id={"sub": front}, device_id_type=MESH)

    @pl.when(has_back)
    def _():
        pl.semaphore_signal(barrier, inc=1, device_id={"sub": back}, device_id_type=MESH)

    def load(which, j):
        part = pl.ds(slab(j), chunk)
        inside = pl.ds(slab(j) + HALO, chunk)
        if which == 0:
            return pltpu.make_async_copy(now_hbm.at[0, part], even.at[inside, inner, :], lsem.at[0, j])
        if which == 1:
            return pltpu.make_async_copy(prev_hbm.at[0, part], odd.at[inside, inner, :], lsem.at[1, j])
        if which == 2:
            return pltpu.make_async_copy(cour_hbm.at[0, part], cour.at[part], lsem.at[2, j])
        return pltpu.make_async_copy(acc_hbm.at[0, :, part], acc.at[:, part], lsem.at[3, j])

    load(0, 0).start()
    load(0, 1).start()
    for j in (1, 0, *range(2, chunks)):
        if 0 < j < chunks - 1:
            load(0, j + 1).start()
        for which in (1, 2, 3):
            load(which, j).start()

    for ref in buf:
        for rim in (0, PAD + rows):
            ref[HALO : HALO + depth, rim : rim + PAD, :] = jnp.zeros((depth, PAD, cols), jnp.float32)

    def clear(first):
        for ref in buf:
            ref[first : first + HALO, inner, :] = jnp.zeros((HALO, rows, cols), jnp.float32)

    @pl.when(jnp.logical_not(has_low))
    def _():
        clear(0)

    @pl.when(jnp.logical_not(has_high))
    def _():
        clear(HALO + depth)

    across = lax.broadcasted_iota(jnp.int32, (cols, cols), 0) - lax.broadcasted_iota(jnp.int32, (cols, cols), 1)
    across = jnp.maximum(across, -across)
    matrix = jnp.where(across == 0, 3.0 * stencil_weights[0], 0.0)
    for d in range(1, 5):
        matrix = jnp.where(across == d, stencil_weights[d], matrix)
    coarse = matrix.astype(jnp.bfloat16)
    along[0:cols] = coarse
    along[cols : 2 * cols] = coarse
    along[2 * cols :] = (matrix - coarse.astype(jnp.float32)).astype(jnp.bfloat16)

    near = jnp.minimum(sub, 1) + jnp.minimum(n_sub - 1 - sub, 1)
    pl.semaphore_wait(barrier, n_shot - 1 + near)

    def halo(t, side):
        b = buf[t % 2]
        if side == 0:
            first, land, device = (1 - rising) * (depth - HALO), rising * (depth + HALO), front
        else:
            first, land, device = rising * (depth - HALO), (1 - rising) * (depth + HALO), back
        source = now_hbm.at[0, pl.ds(first, HALO)] if t == 0 else b.at[pl.ds(first + HALO, HALO), inner, :]
        return pltpu.make_async_remote_copy(
            src_ref=source, dst_ref=b.at[pl.ds(land, HALO), inner, :],
            send_sem=hsend.at[t, side], recv_sem=hrecv.at[t, side],
            device_id={"sub": device}, device_id_type=MESH,
        )

    there = (has_front, has_back)

    def start_halo(t, side):
        @pl.when(there[side])
        def _():
            halo(t, side).start()

    def wait_halo(t, side):
        @pl.when(there[side])
        def _():
            halo(t, side).wait()

    start_halo(0, 0)
    start_halo(0, 1)

    def ids_copy(m):
        peer = peer_of(m)
        return pltpu.make_async_remote_copy(
            src_ref=ids_ref.at[pl.ds(CAP * peer, CAP)], dst_ref=rids.at[pl.ds(CAP * m, CAP)],
            send_sem=isend, recv_sem=irecv, device_id={"shot": peer}, device_id_type=MESH,
        )

    def data_copy(j, m):
        peer = peer_of(m)
        return pltpu.make_async_remote_copy(
            src_ref=packed.at[j, pl.ds(CAP * peer, CAP)], dst_ref=recv.at[j, pl.ds(CAP * m, CAP)],
            send_sem=dsend.at[j], recv_sem=drecv.at[j],
            device_id={"shot": peer}, device_id_type=MESH,
        )

    others = pl.ds(CAP, places - CAP)

    def ids_all():
        return pltpu.make_async_remote_copy(
            src_ref=ids_ref.at[others], dst_ref=rids.at[others],
            send_sem=isend, recv_sem=irecv, device_id={"shot": peer_of(1)}, device_id_type=MESH,
        )

    def data_all(j):
        return pltpu.make_async_remote_copy(
            src_ref=packed.at[j, others], dst_ref=recv.at[j, others],
            send_sem=dsend.at[j], recv_sem=drecv.at[j],
            device_id={"shot": peer_of(1)}, device_id_type=MESH,
        )

    for m in range(1, n_shot):
        ids_copy(m).start()

    def advance(t, j):
        cur, nxt = buf[t % 2], buf[(t + 1) % 2]
        z0 = slab(j)

        def block(i, _):
            column = []
            for u in range(UNROLL):
                here = pl.ds(pl.multiple_of((i * UNROLL + u) * TX + PAD, TX), TX)
                column.append({k: cur[z0 + (k + HALO), here, :] for k in range(-HALO, chunk + HALO)})
            centre = jnp.concatenate([column[u][k] for u in range(UNROLL) for k in range(chunk)], axis=0)
            high = centre.astype(jnp.bfloat16)
            low = (centre - high.astype(jnp.float32)).astype(jnp.bfloat16)
            lap_y = jnp.dot(
                jnp.concatenate([high, low, high], axis=1), along[...], preferred_element_type=jnp.float32
            )
            for u in range(UNROLL):
                xb = i * UNROLL + u
                x0 = pl.multiple_of(xb * TX, TX)
                own = pl.ds(x0, TX)
                here = pl.ds(pl.multiple_of(x0 + PAD, TX), TX)
                col = column[u]
                for k in range(chunk):
                    z = z0 + k
                    c = col[k]
                    n = (u * chunk + k) * TX
                    lap = lap_y[n : n + TX]
                    for d in range(1, 5):
                        pair = (col[k + d] + col[k - d]) + (
                            cur[z + HALO, pl.ds(x0 + (PAD + d), TX), :]
                            + cur[z + HALO, pl.ds(x0 + (PAD - d), TX), :]
                        )
                        lap = lap + stencil_weights[d] * pair
                    source = src_ref[pl.ds((z * rows + x0) * steps + t, TX, stride=steps), :]
                    adv = (2.0 * c - nxt[z + HALO, here, :]) + (cour[z, own, :] * lap + source)
                    if t + 1 < steps:
                        nxt[z + HALO, here, :] = adv
                    else:
                        last[0, z, own, :] = adv
                    g = adv * acc[t, z, own, :]
                    grad[xb, z] = g if t == 0 else grad[xb, z] + g
            return 0

        lax.fori_loop(0, rows // (TX * UNROLL), block, 0)

    def send(j):
        part = pl.ds(slab(j), chunk)

        def pack(p, _):
            packed[j, p] = grad[inv_ref[p], part]
            return 0

        lax.fori_loop(0, places, pack, 0, unroll=4)
        for m in range(1, n_shot):
            data_copy(j, m).start()

    load(0, 0).wait()
    load(0, 1).wait()

    def step(t, j):
        if t == 0:
            @pl.when((j > 0) & (j < chunks - 1))
            def _():
                load(0, j + 1).wait()

            for which in (1, 2, 3):
                load(which, j).wait()

        @pl.when(j == 0)
        def _():
            wait_halo(t, 0)

        @pl.when(j == chunks - 1)
        def _():
            wait_halo(t, 1)

        advance(t, j)
        if t + 1 < steps:
            @pl.when(j == 0)
            def _():
                start_halo(t + 1, 0)

            @pl.when(j == chunks - 1)
            def _():
                start_halo(t + 1, 1)
        else:
            send(j)

    def sweep(i, _):
        many = jnp.where(i == 0, 2, jnp.where(i == 2, 0, jnp.where(i < chunks, 1, 0)))

        def initial(n, _):
            step(0, jnp.where(i == 0, 1 - n, jnp.where(i == 1, 2, i)))
            return 0

        lax.fori_loop(0, many, initial, 0)
        for t in range(1, steps):
            j = i - t

            @pl.when((j >= 0) & (j < chunks))
            def _():
                step(t, j)

        return 0

    lax.fori_loop(0, chunks + steps - 1, sweep, 0)

    far = lax.broadcasted_iota(jnp.int32, taps.shape, 0) - (2 * depth + chunk)
    ratio = 2.0 * far.astype(jnp.float32) / depth
    taps[...] = jnp.where(jnp.maximum(far, -far) <= depth, jnp.exp(-(ratio * ratio)), 0.0)
    row_i = lax.broadcasted_iota(jnp.int32, (depth, 3 * depth), 0)
    row_j = lax.broadcasted_iota(jnp.int32, (depth, 3 * depth), 1) - depth
    gap = row_i - row_j
    whole = row_j + sub * depth
    ratio = 2.0 * gap.astype(jnp.float32) / depth
    valid = (jnp.abs(gap) <= depth) & (whole >= 0) & (whole < n_sub * depth)
    total = jnp.sum(jnp.where(valid, jnp.exp(-(ratio * ratio)), 0.0), axis=1, keepdims=True)
    scale[...] = jnp.broadcast_to(1.0 / total, scale.shape)
    smooth[...] = jnp.zeros(smooth.shape, jnp.float32)

    def spread(first, low, high):
        def row(i, _):
            gap = i - (first - depth) + (2 * depth + chunk)
            w = [taps[gap - k] for k in range(chunk)]
            for g in range(TILES_OWN):
                s = w[0] * tiles[first, g] + w[1] * tiles[first + 1, g]
                for k in range(2, chunk, 2):
                    s = s + (w[k] * tiles[first + k, g] + w[k + 1] * tiles[first + k + 1, g])
                smooth[g, i] += s
            return 0

        lax.fori_loop(low, high, row, 0)

    def collect(j):
        z0 = slab(j)

        def tile(g, _):
            sums = [None] * chunk
            for p in range(places):
                if p < CAP:
                    hit = ids_ref[CAP * shot + p] == g
                    block = [packed[j, CAP * shot + p, k] for k in range(chunk)]
                else:
                    hit = rids[p] == g
                    block = [recv[j, p, k] for k in range(chunk)]
                for k in range(chunk):
                    term = jnp.where(hit, block[k], 0.0)
                    sums[k] = term if sums[k] is None else sums[k] + term
            for k in range(chunk):
                tiles[depth + z0 + k, g] = sums[k]
            return 0

        lax.fori_loop(0, TILES_OWN, tile, 0)

    def pass_on(j, side):
        z0 = slab(j)
        land, device = (2 * depth + z0, sub - 1) if side == 0 else (z0, sub + 1)
        return pltpu.make_async_remote_copy(
            src_ref=tiles.at[pl.ds(depth + z0, chunk)], dst_ref=tiles.at[pl.ds(land, chunk)],
            send_sem=nsend.at[j, side], recv_sem=nrecv.at[j, side],
            device_id={"sub": device}, device_id_type=MESH,
        )

    def finish(j):
        z0 = chunk * (chunks - 1) - slab(j)

        @pl.when(has_low)
        def _():
            pass_on(j, 0).wait_send()
            pass_on(j, 1).wait_recv()
            spread(z0, 0, z0 + chunk)

        @pl.when(has_high)
        def _():
            pass_on(j, 1).wait_send()
            pass_on(j, 0).wait_recv()
            spread(2 * depth + z0, z0, depth)

    ids_all().wait()

    def gather(j):
        data_all(j).wait()
        collect(j)

        @pl.when(has_low)
        def _():
            pass_on(j, 0).start()

        @pl.when(has_high)
        def _():
            pass_on(j, 1).start()

        spread(depth + slab(j), 0, depth)

    def gathers(j, _):
        gather(j)

        @pl.when(j > 0)
        def _():
            finish(j - 1)

        return 0

    lax.fori_loop(0, chunks - 1, gathers, 0)
    finish(chunks - 2)
    gather(chunks - 1)
    finish(chunks - 1)

    def normal(i, _):
        s = scale[pl.ds(i, TX, stride=0), :]
        for g in range(TILES_OWN):
            smooth[g, i] = smooth[g, i] * s
        return 0

    lax.fori_loop(0, depth, normal, 0)


def store_kernel(smooth_ref, last_ref, smooth_hbm, last_hbm, sems):
    copies = [
        pltpu.make_async_copy(last_ref, last_hbm, sems.at[0]),
        pltpu.make_async_copy(smooth_ref, smooth_hbm, sems.at[1]),
    ]
    for c in copies:
        c.start()
    for c in copies:
        c.wait()


def body(courant, adjoint_prev, adjoint_now, forward_accel, traces, receivers, owners, tile_slot):
    n_sub = lax.axis_size("sub")
    n_shot = lax.axis_size("shot")
    _, steps, depth, rows, cols = forward_accel.shape
    places = n_shot * CAP
    chunks = depth // HALO
    f32 = jnp.float32
    smem = pl.BlockSpec(memory_space=pltpu.SMEM)
    vmem = pl.BlockSpec(memory_space=pltpu.VMEM)
    hbm = pl.BlockSpec(memory_space=pl.ANY)

    def in_hbm(x):
        return pltpu.with_memory_space_constraint(x, pltpu.HBM)

    def in_vmem(x):
        return pltpu.with_memory_space_constraint(x, pltpu.VMEM)

    source, inverse, ids = pl.pallas_call(
        functools.partial(prepare_kernel, depth * rows * cols, cols),
        out_shape=(
            pltpu.VMEM(((depth * rows + 2) * steps, cols), f32),
            jax.ShapeDtypeStruct((places,), jnp.int32),
            pltpu.VMEM((places, TX, cols), jnp.int32),
        ),
        in_specs=[hbm] * 4,
        out_specs=(vmem, smem, vmem),
        scratch_shapes=[
            pltpu.SMEM((n_shot,), jnp.int32),
            pltpu.SMEM(receivers.shape, jnp.int32),
            pltpu.VMEM(traces.shape, f32),
            pltpu.SMEM((owners.size,), jnp.int32),
            pltpu.SMEM((tile_slot.size,), jnp.int32),
            pltpu.SemaphoreType.DMA((4,)),
        ],
        compiler_params=pltpu.CompilerParams(vmem_limit_bytes=32 * 2**20),
        name="prepare",
    )(*(in_hbm(x) for x in (receivers, traces, owners.reshape(-1), tile_slot.reshape(-1))))

    last, smoothed = pl.pallas_call(
        functools.partial(adjoint_kernel, n_shot, n_sub),
        out_shape=(
            pltpu.VMEM((1, depth, rows, cols), f32),
            pltpu.VMEM((TILES_OWN, depth, TX, cols), f32),
        ),
        in_specs=[smem, vmem, vmem] + [hbm] * 4,
        out_specs=(vmem, vmem),
        scratch_shapes=[
            pltpu.VMEM((depth + 2 * HALO, rows + 2 * PAD, cols), f32),
            pltpu.VMEM((depth + 2 * HALO, rows + 2 * PAD, cols), f32),
            pltpu.VMEM((depth, rows, cols), f32),
            pltpu.VMEM((steps, depth, rows, cols), f32),
            pltpu.VMEM((rows // TX, depth, TX, cols), f32),
            pltpu.VMEM((chunks, places, HALO, TX, cols), f32),
            pltpu.VMEM((chunks, places, HALO, TX, cols), f32),
            pltpu.VMEM((places, TX, cols), jnp.int32),
            pltpu.VMEM((3 * depth, TILES_OWN, TX, cols), f32),
            pltpu.VMEM((4 * depth + 2 * HALO, TX, cols), f32),
            pltpu.VMEM((depth, cols), f32),
            pltpu.VMEM((3 * cols, cols), jnp.bfloat16),
            pltpu.SemaphoreType.DMA((4, chunks)),
            pltpu.SemaphoreType.DMA((steps, 2)),
            pltpu.SemaphoreType.DMA((steps, 2)),
            pltpu.SemaphoreType.DMA,
            pltpu.SemaphoreType.DMA,
            pltpu.SemaphoreType.DMA((chunks,)),
            pltpu.SemaphoreType.DMA((chunks,)),
            pltpu.SemaphoreType.DMA((chunks, 2)),
            pltpu.SemaphoreType.DMA((chunks, 2)),
        ],
        compiler_params=pltpu.CompilerParams(
            collective_id=0, has_side_effects=True, vmem_limit_bytes=40 * 2**20
        ),
        name="adjoint",
    )(
        inverse, in_vmem(ids), in_vmem(source),
        *(in_hbm(x) for x in (courant, adjoint_prev, adjoint_now, forward_accel)),
    )

    smoothed, last = pl.pallas_call(
        store_kernel,
        out_shape=tuple(pltpu.HBM(x.shape, f32) for x in (smoothed, last)),
        in_specs=[hbm, hbm],
        out_specs=(hbm, hbm),
        scratch_shapes=[pltpu.SemaphoreType.DMA((2,))],
        name="store",
    )(in_vmem(smoothed), in_vmem(last))
    return (smoothed, last)


def solution(mesh):
    placed = (
        P("shot", "sub", None, None),
        P("shot", "sub", None, None),
        P("shot", "sub", None, None),
        P("shot", None, "sub", None, None),
        P("shot", None, None),
        P("shot", None),
        P("shot", "sub", None, None),
        P("shot", "sub", None),
    )
    return jax.shard_map(
        body,
        mesh=mesh,
        in_specs=placed,
        out_specs=(P("shot", "sub", None, None), P("shot", "sub", None, None)),
        check_vma=False,
    )
```
